32 devices in a mesh: dp: 16 (over z, y, core), tensor: 2 (over x).
Axes of the slice: x: 2, y: 2, z: 4, core: 2. Of those that a mesh axis runs over, the one named last changes fastest.
Arguments:
- tokens: bfloat16 [32768, 1024], P(('dp', 'tensor')), may hold values from -6 to 6
- scene_ids: int32 [16, 2048], P('dp'), may hold values from 0 to 3, never falling along the last dimension, each value on 1 to 1024 neighbouring positions
- valid: int32 [16, 2048], P('dp'), may hold values 0 or 1
- norm_gain: bfloat16 [1024], replicated, may hold values from 0.5 to 1.5
- w_z: bfloat16 [1024, 2048], P(None, 'tensor'), may hold values from -0.1875 to 0.1875
- w_x: bfloat16 [1024, 2048], P(None, 'tensor'), may hold values from -0.1875 to 0.1875
- w_b: bfloat16 [1024, 128], replicated, may hold values from -0.1875 to 0.1875
- w_c: bfloat16 [1024, 128], replicated, may hold values from -0.1875 to 0.1875
- w_dt: bfloat16 [1024, 32], P(None, 'tensor'), may hold values from -0.1875 to 0.1875
- conv_x: bfloat16 [4, 2048], P(None, 'tensor'), may hold values from -3 to 3
- conv_x_bias: bfloat16 [2048], P('tensor'), may hold values from -3 to 3
- conv_bc: bfloat16 [4, 256], replicated, may hold values from -3 to 3
- conv_bc_bias: bfloat16 [256], replicated, may hold values from -3 to 3
- dt_bias: bfloat16 [32], P('tensor'), may hold values from -9 to -3.5
- a_log: bfloat16 [32], P('tensor'), may hold values from 0 to 2.765625
- d_skip: bfloat16 [32], P('tensor'), may hold values from 0.5 to 1.5
- gate_gain: bfloat16 [2048], P('tensor'), may hold values from 0.5 to 1.5
- w_out: bfloat16 [2048, 1024], P('tensor'), may hold values from -0.125 to 0.125
- cotangent: bfloat16 [32768, 1024], P(('dp', 'tensor')), may hold values from -6 to 6
Outputs:
- block_out: bfloat16 [32768, 1024], P(('dp', 'tensor'))
- grad_tokens: bfloat16 [32768, 1024], P(('dp', 'tensor'))
- grad_norm_gain: float32 [1024], replicated
- grad_w_z: float32 [1024, 2048], P(None, 'tensor')
- grad_w_x: float32 [1024, 2048], P(None, 'tensor')
- grad_w_b: float32 [1024, 128], replicated
- grad_w_c: float32 [1024, 128], replicated
- grad_w_dt: float32 [1024, 32], P(None, 'tensor')
- grad_conv_x: float32 [4, 2048], P(None, 'tensor')
- grad_conv_x_bias: float32 [2048], P('tensor')
- grad_conv_bc: float32 [4, 256], replicated
- grad_conv_bc_bias: float32 [256], replicated
- grad_dt_bias: float32 [32], P('tensor')
- grad_a_log: float32 [32], P('tensor')
- grad_d_skip: float32 [32], P('tensor')
- grad_gate_gain: float32 [2048], P('tensor')
- grad_w_out: float32 [2048, 1024], P('tensor')
The draws below stay inside these ranges and needn't reach their ends.
Inputs may be any that keep to these rules, and one draw needn't show every extreme that they name: `scene_ids`: each packed row of 2048 holds 4 scenes one after another, numbered from 0 up, each of 1 to 1024 rows, one of exactly 1024.
All inputs are finite; a program needn't handle non-finite values. No bound on the sum of `valid` on one device may be relied on, other than what follows from the above.
Results may differ from the reference program's by a relative error of at most 0.0081.
Values may be sent and summed in bfloat16 or wider, within the bound.
No kernel may reach another device: no remote copies, remote signals or barrier semaphores. Data moves between devices by JAX's collectives and lax.ppermute only.
A program may use at most 256 MiB of HBM per device.

```python
import math
import jax
import jax.numpy as jnp
import numpy as np
from jax import lax

D = 1024
H = 32
N = 128
K = 4
TOK_DEV = 2048
SCENES = 4
SPAN = 512
E = 2048
SCENE_MOST = 1024
PACKS = 16
TOKENS = 32768


def set_ends(entries, stream_key, low, top_value):
    place = [jax.random.randint(jax.random.fold_in(stream_key, axis), (), 0, length) for axis, length in enumerate(entries.shape)]
    widest = entries.shape.index(max(entries.shape))
    neighbour = place[:widest] + [(place[widest] + 1) % entries.shape[widest]] + place[widest + 1:]
    return entries.at[tuple(place)].set(low).at[tuple(neighbour)].set(top_value)


def levels(stream_key, dims, shards, least, largest):
    factor_of, own = 1.0, jax.random.fold_in(stream_key, 6)
    for position, parts in shards:
        steps = jnp.exp(jax.random.uniform(jax.random.fold_in(own, position), (parts,), jnp.float32, least / len(shards), largest / len(shards)))
        factor_of = factor_of * jnp.repeat(steps, dims[position] // parts).reshape([-1 if axis == position else 1 for axis in range(len(dims))])
    return factor_of


def split_up(amount, total, bound, skew):
    portions = [(1 << 20) // math.isqrt(rank ** skew) + 1 for rank in range(2, amount + 1)]
    spare, counts = total - bound - (amount - 1), [1] * (amount - 1)
    while spare > 0:
        candidates = [i for i in range(amount - 1) if counts[i] < bound]
        whole, remaining = sum([portions[i] for i in candidates]), spare
        for i in candidates:
            extra = min(bound - counts[i], max(1, remaining * portions[i] // whole), spare)
            counts[i] = counts[i] + extra
            spare = spare - extra
    return np.array([bound] + counts)


def ragged(rng, amount, total, bound, skew):
    if amount == 2:
        one = jax.random.randint(rng, (), max(1, total - bound), min(bound, total - 1) + 1)
        return jnp.stack([one, total - one])
    lengths = jnp.asarray(split_up(amount, total, bound, skew), jnp.int32)
    pairs = (amount - 1) // 2
    source_of, sink = lengths[1:1 + 2 * pairs:2], lengths[2:2 + 2 * pairs:2]
    margin = jnp.minimum(source_of - 1, bound - sink)
    moved = jax.random.randint(jax.random.fold_in(rng, 1), (pairs,), 0, 1 << 20) % (margin + 1)
    lengths = lengths.at[1:1 + 2 * pairs:2].set(source_of - moved).at[2:2 + 2 * pairs:2].set(sink + moved)
    return lengths[jax.random.permutation(jax.random.fold_in(rng, 2), amount)]


def scatter_about(stream_key, extent, scale, bound, cuts=(), held_as=jnp.bfloat16):
    drawn = jax.random.normal(stream_key, extent, jnp.float32) * scale
    if len(cuts) > 0:
        drawn = levels(stream_key, extent, cuts, -0.22, 0.18) * drawn
    return jnp.clip(drawn, min=-bound, max=bound).astype(held_as)


def setup_inputs(seed: int = 0) -> dict:
    splits = jax.random.split(jax.random.key(seed), 20)
    tokens = scatter_about(splits[0], (TOKENS, D), 1.0, 6.0, ((0, 32),))
    scene_ids = jax.vmap(lambda own: jnp.searchsorted(jnp.cumsum(ragged(own, SCENES, TOK_DEV, SCENE_MOST, 2)), jnp.arange(TOK_DEV), side="right"))(jax.random.split(splits[1], PACKS)).reshape((PACKS, TOK_DEV)).astype(jnp.int32)
    valid = set_ends((jax.random.randint(splits[2], (PACKS, TOK_DEV), 0, 8) < 7).astype(jnp.int32), jax.random.fold_in(splits[2], 1), 0, 1)
    norm_gain = jnp.clip(1.0 + 0.1 * jax.random.normal(splits[3], (D,), jnp.float32), 0.5, 1.5).astype(jnp.bfloat16)
    w_z = scatter_about(splits[4], (D, E), D ** -0.5, 0.1875, ((1, 2),))
    w_x = scatter_about(splits[5], (D, E), D ** -0.5, 0.1875, ((1, 2),))
    w_b = scatter_about(splits[6], (D, N), D ** -0.5, 0.1875)
    w_c = scatter_about(splits[7], (D, N), D ** -0.5, 0.1875)
    w_dt = scatter_about(splits[8], (D, H), D ** -0.5, 0.1875, ((1, 2),))
    conv_x = scatter_about(splits[9], (K, E), K ** -0.5, 3.0, ((1, 2),))
    conv_x_bias = scatter_about(splits[10], (E,), 0.5, 3.0, ((0, 2),))
    conv_bc = scatter_about(splits[11], (K, 2 * N), K ** -0.5, 3.0)
    conv_bc_bias = scatter_about(splits[12], (2 * N,), 0.5, 3.0)
    dt_bias = jnp.clip(-9.0 + 5.5 * jax.random.uniform(splits[13], (H,), jnp.float32) ** levels(splits[13], (H,), ((0, 2),), -0.2, 0.2), -9.0, -3.5).astype(jnp.bfloat16)
    a_log = jnp.clip(2.765625 * jax.random.uniform(splits[14], (H,), jnp.float32) ** levels(splits[14], (H,), ((0, 2),), -0.2, 0.2), 0.0, 2.765625).astype(jnp.bfloat16)
    d_skip = jnp.clip(0.5 + 1.0 * jax.random.uniform(splits[15], (H,), jnp.float32) ** levels(splits[15], (H,), ((0, 2),), -0.2, 0.2), 0.5, 1.5).astype(jnp.bfloat16)
    gate_gain = jnp.clip(1.0 + 0.1 * jax.random.normal(splits[16], (E,), jnp.float32), 0.5, 1.5).astype(jnp.bfloat16)
    w_out = scatter_about(splits[17], (E, D), E ** -0.5, 0.125, ((0, 2),))
    cotangent = scatter_about(splits[18], (TOKENS, D), 1.0, 6.0, ((0, 32),))
    return dict(tokens=tokens, scene_ids=scene_ids, valid=valid, norm_gain=norm_gain, w_z=w_z, w_x=w_x, w_b=w_b, w_c=w_c, w_dt=w_dt, conv_x=conv_x, conv_x_bias=conv_x_bias, conv_bc=conv_bc, conv_bc_bias=conv_bc_bias, dt_bias=dt_bias, a_log=a_log, d_skip=d_skip, gate_gain=gate_gain, w_out=w_out, cotangent=cotangent)


EPSILON = 1e-05

@jax.custom_vjp
def low(v):
    return lax.optimization_barrier(v.astype(jnp.bfloat16)).astype(jnp.float32)

@jax.custom_vjp
def low_back(v):
    return v

def low_keep(v):
    return (low(v), None)

def low_pass(kept, grad):
    return (grad,)

def back_keep(v):
    return (v, None)

def back_low(kept, grad):
    return (low(grad),)
low.defvjp(low_keep, low_pass)
low_back.defvjp(back_keep, back_low)

def causal_conv(values, kernel, bias_row, scene_row):
    tap_count = kernel.shape[0]
    result = bias_row[None, :] + kernel[tap_count - 1][None, :] * values
    for lag_rows in range(1, tap_count):
        shifted = jnp.pad(values[:-lag_rows], ((lag_rows, 0), (0, 0)))
        earlier = jnp.pad(scene_row[:-lag_rows], (lag_rows, 0), constant_values=-1)
        same_scene = (earlier == scene_row).astype(jnp.float32)[:, None]
        result = result + kernel[tap_count - 1 - lag_rows][None, :] * shifted * same_scene
    return result

def ssd_scan(x_heads, dt_step, log_decay, b_matrix, c_matrix, scene_row, d_skip):
    row_total, head_count, head_width = x_heads.shape
    block_count = row_total // SPAN
    highest = lax.Precision.HIGHEST

    def block_step(carry_pair, block_items):
        carried_state, prev_seg = carry_pair
        x_block, step_block, decay_block, b_block, c_block, seg_block = block_items
        cumulative = jnp.cumsum(decay_block, axis=0)
        positions = jnp.arange(SPAN)
        causal_mask = (positions[:, None] >= positions[None, :]) & (seg_block[:, None] == seg_block[None, :])
        log_gap = cumulative[:, None, :] - cumulative[None, :, :]
        weight = jnp.where(causal_mask[:, :, None], jnp.exp(jnp.where(causal_mask[:, :, None], log_gap, 0.0)), 0.0)
        scores = jnp.dot(c_block, b_block.T, precision=highest)
        mixing = weight * scores[:, :, None] * step_block[None, :, :]
        inner_part = jnp.einsum('ijh,jhp->ihp', mixing, x_block, precision=highest)
        carried = (seg_block == prev_seg).astype(jnp.float32)
        from_state = jnp.einsum('in,hnp->ihp', c_block, carried_state, precision=highest)
        from_state = from_state * (jnp.exp(cumulative) * carried[:, None])[:, :, None]
        block_out = inner_part + from_state + d_skip[None, :, None] * x_block
        last_seg = seg_block[-1]
        tail_weight = jnp.exp(cumulative[-1][None, :] - cumulative) * step_block * (seg_block == last_seg).astype(jnp.float32)[:, None]
        keep_factor = jnp.exp(cumulative[-1]) * (last_seg == prev_seg).astype(jnp.float32)
        new_state = keep_factor[:, None, None] * carried_state + jnp.einsum('jh,jn,jhp->hnp', tail_weight, b_block, x_block, precision=highest)
        return ((new_state, last_seg), block_out)
    state_init = jnp.zeros((head_count, b_matrix.shape[1], head_width), jnp.float32)
    block_items = (x_heads.reshape(block_count, SPAN, head_count, head_width), dt_step.reshape(block_count, SPAN, head_count), log_decay.reshape(block_count, SPAN, head_count), b_matrix.reshape(block_count, SPAN, -1), c_matrix.reshape(block_count, SPAN, -1), scene_row.reshape(block_count, SPAN))
    final_pair, outputs = lax.scan(jax.checkpoint(block_step), (state_init, jnp.array(-1, jnp.int32)), block_items)
    return outputs.reshape(row_total, head_count, head_width)

def mixer(x_raw, bc_raw, dt_raw, conv_x, conv_x_bias, conv_bc, conv_bc_bias, dt_bias, a_log, d_skip, scene_row, live_row):
    x_conv = jax.nn.silu(causal_conv(x_raw, conv_x, conv_x_bias, scene_row)) * live_row[:, None]
    bc_conv = jax.nn.silu(causal_conv(bc_raw, conv_bc, conv_bc_bias, scene_row))
    half_state = bc_conv.shape[1] // 2
    dt_step = jax.nn.softplus(dt_raw + dt_bias[None, :]) * live_row[:, None]
    log_decay = -jnp.exp(a_log)[None, :] * dt_step
    head_count = dt_raw.shape[1]
    x_heads = x_conv.reshape(x_conv.shape[0], head_count, -1)
    mixed = ssd_scan(x_heads, dt_step, log_decay, bc_conv[:, :half_state], bc_conv[:, half_state:], scene_row, d_skip)
    return mixed.reshape(x_conv.shape[0], -1)

def block_forward(resid, norm_gain, w_z, w_x, w_b, w_c, w_dt, conv_x, conv_x_bias, conv_bc, conv_bc_bias, dt_bias, a_log, d_skip, gate_gain, w_out, scene_row, live_row):
    highest = lax.Precision.HIGHEST
    inverse_in = lax.rsqrt(lax.optimization_barrier(jnp.mean(resid * resid, axis=1, keepdims=True)) + EPSILON)
    normed = low(resid * inverse_in * norm_gain[None, :])
    gate_raw = low_back(jnp.dot(normed, w_z, precision=highest))
    x_raw = low_back(jnp.dot(normed, w_x, precision=highest))
    bc_raw = low_back(jnp.dot(normed, jnp.concatenate([w_b, w_c], axis=1), precision=highest))
    dt_raw = low_back(jnp.dot(normed, w_dt, precision=highest))
    mixed = mixer(x_raw, bc_raw, dt_raw, conv_x, conv_x_bias, conv_bc, conv_bc_bias, dt_bias, a_log, d_skip, scene_row, live_row)
    gated = mixed * jax.nn.silu(gate_raw)
    inverse_gate = lax.rsqrt(lax.optimization_barrier(jnp.mean(gated * gated, axis=1, keepdims=True)) + EPSILON)
    normed_gate = low(gated * inverse_gate * gate_gain[None, :])
    branch = low_back(jnp.dot(normed_gate, w_out, precision=highest))
    return resid + live_row[:, None] * branch

def reference(tokens, scene_ids, valid, norm_gain, w_z, w_x, w_b, w_c, w_dt, conv_x, conv_x_bias, conv_bc, conv_bc_bias, dt_bias, a_log, d_skip, gate_gain, w_out, cotangent):
    weights = tuple((member.astype(jnp.float32) for member in (norm_gain, w_z, w_x, w_b, w_c, w_dt, conv_x, conv_x_bias, conv_bc, conv_bc_bias, dt_bias, a_log, d_skip, gate_gain, w_out)))
    pack_tokens = tokens.reshape(PACKS, TOK_DEV, D)
    pack_cot = cotangent.reshape(PACKS, TOK_DEV, D)

    def one_pack(totals, pack_items):
        rows_in, scene_row, valid_row, cot_rows = pack_items
        live_row = valid_row.astype(jnp.float32)

        def forward(resid, *params):
            return block_forward(resid, *params, scene_row, live_row)
        outputs, pullback = jax.vjp(forward, rows_in.astype(jnp.float32), *weights)
        gradients = pullback(cot_rows.astype(jnp.float32))
        totals = tuple((running + gradient for running, gradient in zip(totals, gradients[1:])))
        return (totals, (outputs.astype(jnp.bfloat16), gradients[0].astype(jnp.bfloat16)))
    zeros_init = tuple((jnp.zeros_like(member) for member in weights))
    totals, (outputs, input_grad) = lax.scan(one_pack, zeros_init, (pack_tokens, scene_ids, valid, pack_cot))
    g_norm, g_wz, g_wx, g_wb, g_wc, g_wdt, g_convx, g_convxb, g_convbc, g_convbcb, g_dtb, g_alog, g_dskip, g_gate, g_wout = totals
    return (outputs.reshape(TOKENS, D), input_grad.reshape(TOKENS, D), g_norm, g_wz, g_wx, g_wb, g_wc, g_wdt, g_convx, g_convxb, g_convbc, g_convbcb, g_dtb, g_alog, g_dskip, g_gate, g_wout)
```

```python
import functools

import jax
import jax.numpy as jnp
from jax import lax
from jax.experimental import pallas as pl
from jax.experimental.pallas import tpu as pltpu
from jax.sharding import PartitionSpec as P

EPSILON = 1e-05
HEAD = 64
LANES = 128
CHUNK = 128
TAPS = 4
FAR = -1e30
F32 = jnp.float32
BF16 = jnp.bfloat16
HIGHEST = lax.Precision.HIGHEST

LIVE, PREV, NEXT, SCENE, CARRIED, TAIL, KEEP = 0, 1, 4, 7, 8, 9, 10


def nn(left, right):
    return jnp.dot(left, right, preferred_element_type=F32)


def nt(left, right):
    return lax.dot_general(left, right, (((1,), (1,)), ((), ())), preferred_element_type=F32)


def split(value):
    high = value.astype(BF16)
    return high, (value - high.astype(F32)).astype(BF16)


def fine(product, left, right):
    left_high, left_low = split(left)
    right_high, right_low = split(right)
    return product(left_high, right_high) + (product(left_high, right_low) + product(left_low, right_high))


def tn(left, right):
    return lax.dot_general(left, right, (((0,), (0,)), ((), ())), preferred_element_type=F32)


def sigmoid(value):
    return 1.0 / (1.0 + jnp.exp(-value))


def softplus(value):
    small = jnp.exp(-jnp.abs(value))
    shifted = 1.0 + small
    tiny = shifted == 1.0
    ratio = jnp.log(shifted) * small / jnp.where(tiny, 1.0, shifted - 1.0)
    return jnp.maximum(value, 0.0) + jnp.where(tiny, small, ratio)


def spread(rows, table):
    high, low = split(rows)
    return nn(high, table) + nn(low, table)


def fold8(value):
    return jnp.sum(value.reshape(value.shape[0] // 8, 8, value.shape[1]), axis=0)


def head_pair(value):
    lane = lax.broadcasted_iota(jnp.int32, value.shape, 1)
    zero = jnp.zeros_like(value)
    return jnp.concatenate(
        [jnp.where(lane < HEAD, value, zero), jnp.where(lane < HEAD, zero, value)], axis=0
    )


def forward_kernel(
    per_block, at_ref, mine_ref, other_ref, zmine_ref, zother_ref, col_ref, row_ref, kx_ref, kbc_ref, hp_ref, ex_ref,
    gated_ref, silu_ref, slope_ref, xc_ref, sp_ref, raw_ref, bc_ref, spbc_ref, dt_ref, cum_ref, ds_ref, sq_ref, st_ref,
    xs, gs, state,
):
    rows, width = xc_ref.shape
    double = bc_ref.shape[1]
    count = double // 2
    own = pl.program_id(0) // per_block == at_ref[0]

    @pl.when(pl.program_id(0) == 0)
    def _():
        xs[0:8, :] = jnp.zeros((8, xs.shape[1]), F32)
        state[...] = jnp.zeros_like(state)

    @pl.when(own)
    def _():
        xs[8:, :] = mine_ref[...]
        gs[...] = zmine_ref[...]

    @pl.when(jnp.logical_not(own))
    def _():
        xs[8:, :] = other_ref[...]
        gs[...] = zother_ref[...]

    raw_ref[...] = xs[8:, : width + double].astype(BF16)
    live = col_ref[:, LIVE : LIVE + 1]
    same = [col_ref[:, PREV + lag : PREV + lag + 1] for lag in range(TAPS - 1)]

    side = slice(width, width + double)
    raw = xs[8:, side]
    pre = kbc_ref[TAPS : TAPS + 1, :] + kbc_ref[TAPS - 1 : TAPS, :] * raw
    for lag in range(1, TAPS):
        tap = kbc_ref[TAPS - 1 - lag : TAPS - lag, :]
        pre = pre + tap * (xs[8 - lag : 8 - lag + rows, side] * same[lag - 1])
    sig = sigmoid(pre)
    act = pre * sig
    spbc_ref[...] = (sig * (1.0 + pre * (1.0 - sig))).astype(spbc_ref.dtype)
    bc_ref[...] = act
    act16 = act.astype(BF16)
    b16 = act16[:, :count]
    c16 = act16[:, count:]

    biased = xs[8:, width + double :] + hp_ref[0:1, :]
    ds_ref[...] = sigmoid(biased) * live
    step = softplus(biased) * live
    dt_ref[...] = step
    decay = step * hp_ref[1:2, :]
    above = lax.broadcasted_iota(jnp.int32, (rows, rows), 0)
    along = lax.broadcasted_iota(jnp.int32, (rows, rows), 1)
    lower = above >= along
    cum = jnp.dot(lower.astype(F32), decay, precision=HIGHEST, preferred_element_type=F32)
    cum_ref[...] = cum
    cum_t = cum.T
    last = cum[rows - 1 : rows, :]
    from_start = jnp.exp(cum) * col_ref[:, CARRIED : CARRIED + 1]
    to_end = jnp.exp(last - cum) * col_ref[:, TAIL : TAIL + 1]
    keep = jnp.exp(last) * col_ref[0:1, KEEP : KEEP + 1]
    table = ex_ref[...]
    wide = spread(jnp.concatenate([step, from_start, to_end, jnp.broadcast_to(keep, (8, LANES))], axis=0), table)

    mask = lower & (col_ref[:, SCENE : SCENE + 1] == row_ref[0:1, :])
    scores = nt(c16, b16)
    b_t = act[:, :count].T
    squares = jnp.zeros((rows, LANES), F32)
    for group in range(width // LANES):
        part = slice(group * LANES, (group + 1) * LANES)
        pre = kx_ref[TAPS : TAPS + 1, part] + kx_ref[TAPS - 1 : TAPS, part] * xs[8:, part]
        for lag in range(1, TAPS):
            tap = kx_ref[TAPS - 1 - lag : TAPS - lag, part]
            pre = pre + tap * (xs[8 - lag : 8 - lag + rows, part] * same[lag - 1])
        sig = sigmoid(pre)
        xc = pre * sig * live
        xc_ref[:, part] = xc
        sp_ref[:, part] = (sig * (1.0 + pre * (1.0 - sig)) * live).astype(BF16)
        both = []
        for head in (2 * group, 2 * group + 1):
            gap = cum[:, head : head + 1] - cum_t[head : head + 1, :]
            weight = jnp.exp(jnp.where(mask, gap, FAR))
            both.append((weight * scores).astype(BF16))
        stepped = xc * wide[:rows, part]
        inner = nn(jnp.concatenate(both, axis=1), head_pair(stepped.astype(BF16)))
        old = state[:, part]
        old16 = old.astype(BF16)
        st_ref[0, :, part] = old
        mixed = inner + nn(c16, old16) * wide[rows : 2 * rows, part] + kx_ref[TAPS + 1 : TAPS + 2, part] * xc
        fed = stepped * wide[2 * rows : 3 * rows, part]
        state[:, part] = old * wide[3 * rows : 3 * rows + 1, part] + fine(nn, b_t, fed)
        gate = gs[:, part]
        sig = sigmoid(gate)
        silu = gate * sig
        gated = mixed * silu
        gated_ref[:, part] = (gated * kx_ref[TAPS + 2 : TAPS + 3, part]).astype(BF16)
        silu_ref[:, part] = silu.astype(BF16)
        slope_ref[:, part] = (mixed * sig * (1.0 + gate * (1.0 - sig))).astype(BF16)
        squares = squares + gated * gated
    sq_ref[...] = nt(jnp.ones((8, LANES), BF16), squares.astype(BF16))
    xs[0:8, :] = xs[rows : rows + 8, :]


def backward_kernel(
    at_ref, dy_ref, xc_ref, sp_ref, x_ref, bc_ref, spbc_ref, dt_ref, cum_ref, ds_ref, col_ref, row_ref,
    st_ref, kx_ref, kbc_ref, hp_ref, ex_ref, fo_ref,
    out_ref, gk_ref, gkbc_ref, gh_ref,
    dvs, dbs, grad, rowsum,
):
    rows, width = xc_ref.shape
    double = bc_ref.shape[1]
    count = double // 2

    @pl.when(pl.program_id(0) == 0)
    def _():
        dvs[rows:, :] = jnp.zeros((8, width), F32)
        dbs[rows:, :] = jnp.zeros((8, double), F32)
        grad[...] = jnp.zeros_like(grad)
        rowsum[...] = jnp.zeros_like(rowsum)
        gk_ref[...] = jnp.zeros_like(gk_ref)
        gkbc_ref[...] = jnp.zeros_like(gkbc_ref)
        gh_ref[...] = jnp.zeros_like(gh_ref)

    @pl.when(pl.program_id(0) > 0)
    def _():
        dvs[rows:, :] = dvs[0:8, :]
        dbs[rows:, :] = dbs[0:8, :]

    same = [col_ref[:, NEXT + lag : NEXT + lag + 1] for lag in range(TAPS - 1)]
    b = bc_ref[:, :count]
    c = bc_ref[:, count:]
    step = dt_ref[...]
    cum = cum_ref[...]
    cum_t = cum.T
    last = cum[rows - 1 : rows, :]
    from_start = jnp.exp(cum) * col_ref[:, CARRIED : CARRIED + 1]
    to_end = jnp.exp(last - cum) * col_ref[:, TAIL : TAIL + 1]
    keep = jnp.exp(last) * col_ref[0:1, KEEP : KEEP + 1]
    table = ex_ref[...]
    wide = spread(jnp.concatenate([step, from_start, to_end, jnp.broadcast_to(keep, (8, LANES))], axis=0), table)

    above = lax.broadcasted_iota(jnp.int32, (rows, rows), 0)
    along = lax.broadcasted_iota(jnp.int32, (rows, rows), 1)
    upper = above <= along
    mask = upper & (col_ref[:, SCENE : SCENE + 1] == row_ref[0:1, :])
    scores = fine(nt, b, c)
    c_t = c.T
    lane = lax.broadcasted_iota(jnp.int32, (rows, LANES), 1)

    d_scores = jnp.zeros((rows, rows), F32)
    d_b = jnp.zeros((rows, count), F32)
    d_c = jnp.zeros((rows, count), F32)
    d_cum = jnp.zeros((rows, LANES), F32)
    d_step = jnp.zeros((rows, LANES), F32)
    d_last = jnp.zeros((8, LANES), F32)
    for group in range(width // LANES):
        part = slice(group * LANES, (group + 1) * LANES)
        dy = dy_ref[:, part]
        xc = xc_ref[:, part]
        wide_step = wide[:rows, part]
        wide_end = wide[2 * rows : 3 * rows, part]
        fold = fo_ref[part, :]
        pair = head_pair(dy)
        stepped = xc * wide_step
        back = fine(nt, stepped, pair)
        both = []
        for which, head in enumerate((2 * group, 2 * group + 1)):
            gap = cum_t[head : head + 1, :] - cum[:, head : head + 1]
            weight = jnp.exp(jnp.where(mask, gap, FAR))
            both.append(weight * scores)
            weighted = back[:, which * rows : (which + 1) * rows] * weight
            d_scores = d_scores + weighted
            inner = weighted * scores
            rowsum[head : head + 1, :] = jnp.sum(inner, axis=0, keepdims=True)
            d_cum = d_cum - jnp.where(lane == head, jnp.sum(inner, axis=1, keepdims=True), 0.0)
        d_stepped = fine(nn, jnp.concatenate(both, axis=1), pair)
        old = st_ref[0, :, part]
        after = grad[:, part]
        carried = dy * wide[rows : 2 * rows, part]
        fed = stepped * wide_end
        from_after = fine(nn, b, after)
        to_last = fed * from_after
        d_b = d_b + fine(nt, fed, after)
        d_c = d_c + fine(nt, carried, old)
        d_cum = d_cum + spread(carried * fine(nn, c, old) - to_last, fold)
        kept = wide[3 * rows : 3 * rows + 1, part]
        total = fold8(to_last) + fold8(after * old) * kept
        d_last = d_last + spread(total, fold)
        grad[:, part] = after * kept + fine(nn, c_t, carried)
        d_stepped = d_stepped + from_after * wide_end
        d_xc = d_stepped * wide_step + kx_ref[TAPS + 1 : TAPS + 2, part] * dy
        d_step = d_step + spread(d_stepped * xc, fold)
        dv = d_xc * sp_ref[:, part].astype(F32)
        dvs[0:rows, part] = dv
        x = x_ref[:, part].astype(F32)
        xg = kx_ref[TAPS - 1 : TAPS, part] * dv
        gk_ref[8 * (TAPS - 1) : 8 * TAPS, part] += fold8(x * dv)
        gk_ref[8 * TAPS : 8 * TAPS + 8, part] += fold8(dv)
        gk_ref[8 * TAPS + 8 : 8 * TAPS + 16, part] += fold8(dy * xc)
        for lag in range(1, TAPS):
            moved = dvs[lag : lag + rows, part] * same[lag - 1]
            xg = xg + kx_ref[TAPS - 1 - lag : TAPS - lag, part] * moved
            gk_ref[8 * (TAPS - 1 - lag) : 8 * (TAPS - lag), part] += fold8(x * moved)
        out_ref[:, part] = xg.astype(BF16)

    d_b = d_b + fine(nn, d_scores, c)
    d_c = d_c + fine(nn, d_scores.T, b)
    for side, value in ((0, d_b), (1, d_c)):
        part = slice(side * count, (side + 1) * count)
        dv = value * spbc_ref[:, part].astype(F32)
        dbs[0:rows, part] = dv
        raw = x_ref[:, width + side * count : width + (side + 1) * count].astype(F32)
        out = kbc_ref[TAPS - 1 : TAPS, part] * dv
        gkbc_ref[8 * (TAPS - 1) : 8 * TAPS, part] += fold8(raw * dv)
        gkbc_ref[8 * TAPS : 8 * TAPS + 8, part] += fold8(dv)
        for lag in range(1, TAPS):
            moved = dbs[lag : lag + rows, part] * same[lag - 1]
            out = out + kbc_ref[TAPS - 1 - lag : TAPS - lag, part] * moved
            gkbc_ref[8 * (TAPS - 1 - lag) : 8 * (TAPS - lag), part] += fold8(raw * moved)
        out_ref[:, width + side * count : width + (side + 1) * count] = out.astype(BF16)

    d_cum = d_cum + rowsum[...].T
    d_decay = jnp.dot(upper.astype(F32), d_cum, precision=HIGHEST, preferred_element_type=F32)
    d_decay = d_decay + jnp.sum(d_last, axis=0, keepdims=True)
    d_step = d_step + d_decay * hp_ref[1:2, :]
    d_raw = d_step * ds_ref[...]
    gh_ref[0:8, :] += fold8(d_raw)
    gh_ref[8:16, :] += fold8(d_decay * step * hp_ref[1:2, :])
    out_ref[:, width + double :] = d_raw.astype(BF16)


def physical(step, at, size, per_block):
    return lax.rem(at - step // per_block + size, size) * per_block + lax.rem(step, per_block)


def call_forward(at, size, mine, other, zmine, zother, col, row, kx, kbc, hp, expand):
    cat = mine.shape[1]
    width = zmine.shape[1]
    double = cat - width - LANES
    total = mine.shape[0] * size
    steps = total // CHUNK
    per_block = mine.shape[0] // CHUNK

    def own_place(i, at_ref):
        return jnp.clip(i - at_ref[0] * per_block, 0, per_block - 1), 0

    def other_place(i, at_ref):
        place = physical(i, at_ref[0], size, per_block) - per_block
        resting = jnp.where(at_ref[0] == 0, (size - 2) * per_block, per_block - 1)
        return jnp.where(place < 0, resting, place), 0

    def rows(cols):
        return pl.BlockSpec((CHUNK, cols), lambda i, at_ref: (i, 0))

    def moved(cols):
        return pl.BlockSpec((CHUNK, cols), lambda i, at_ref: (physical(i, at_ref[0], size, per_block), 0))

    def whole(array):
        return pl.BlockSpec(array.shape, lambda i, at_ref: (0, 0))

    lanes8 = pl.BlockSpec((8, CHUNK), lambda i, at_ref: (0, i))
    shape = jax.ShapeDtypeStruct
    return pl.pallas_call(
        functools.partial(forward_kernel, per_block),
        grid_spec=pltpu.PrefetchScalarGridSpec(
            num_scalar_prefetch=1,
            grid=(steps,),
            in_specs=[
                pl.BlockSpec((CHUNK, cat), own_place), pl.BlockSpec((CHUNK, cat), other_place),
                pl.BlockSpec((CHUNK, width), own_place), pl.BlockSpec((CHUNK, width), other_place),
                rows(LANES), lanes8, whole(kx), whole(kbc), whole(hp), whole(expand),
            ],
            out_specs=[
                moved(width), moved(width), moved(width), rows(width), rows(width), rows(width + double),
                rows(double), rows(double), rows(LANES), rows(LANES), rows(LANES), lanes8,
                pl.BlockSpec((1, double // 2, width), lambda i, at_ref: (i, 0, 0)),
            ],
            scratch_shapes=[
                pltpu.VMEM((CHUNK + 8, cat), F32),
                pltpu.VMEM((CHUNK, width), F32),
                pltpu.VMEM((double // 2, width), F32),
            ],
        ),
        out_shape=[
            shape((total, width), BF16), shape((total, width), BF16), shape((total, width), BF16),
            shape((total, width), F32), shape((total, width), BF16), shape((total, width + double), BF16),
            shape((total, double), F32), shape((total, double), BF16),
            shape((total, LANES), F32), shape((total, LANES), F32), shape((total, LANES), F32), shape((8, total), F32),
            shape((steps, double // 2, width), F32),
        ],
        name="scan_forward",
    )(at, mine, other, zmine, zother, col, row, kx, kbc, hp, expand)


def call_backward(at, size, dy, xc, sp, raw, bc, spbc, step, cum, dsig, col, row, states, kx, kbc, hp, expand, fold):
    total, width = xc.shape
    double = bc.shape[1]
    cat = width + double + LANES
    steps = total // CHUNK
    per_block = steps // size

    def rows(cols):
        return pl.BlockSpec((CHUNK, cols), lambda i, at_ref: (steps - 1 - i, 0))

    def moved(cols):
        return pl.BlockSpec((CHUNK, cols), lambda i, at_ref: (physical(steps - 1 - i, at_ref[0], size, per_block), 0))

    def whole(array):
        return pl.BlockSpec(array.shape, lambda i, at_ref: (0, 0))

    lanes8 = pl.BlockSpec((8, CHUNK), lambda i, at_ref: (0, steps - 1 - i))
    shape = jax.ShapeDtypeStruct
    sums = [shape((8 * (TAPS + 2), width), F32), shape((8 * (TAPS + 1), double), F32), shape((16, LANES), F32)]
    return pl.pallas_call(
        backward_kernel,
        grid_spec=pltpu.PrefetchScalarGridSpec(
            num_scalar_prefetch=1,
            grid=(steps,),
            in_specs=[
                moved(width), rows(width), rows(width), rows(width + double),
                rows(double), rows(double), rows(LANES), rows(LANES), rows(LANES), rows(LANES), lanes8,
                pl.BlockSpec((1, double // 2, width), lambda i, at_ref: (steps - 1 - i, 0, 0)),
                whole(kx), whole(kbc), whole(hp), whole(expand), whole(fold),
            ],
            out_specs=[moved(cat)] + [whole(member) for member in sums],
            scratch_shapes=[
                pltpu.VMEM((CHUNK + 8, width), F32),
                pltpu.VMEM((CHUNK + 8, double), F32),
                pltpu.VMEM((double // 2, width), F32),
                pltpu.VMEM((LANES, CHUNK), F32),
            ],
        ),
        out_shape=[shape((total, cat), BF16)] + sums,
        name="scan_backward",
    )(at, dy, xc, sp, raw, bc, spbc, step, cum, dsig, col, row, states, kx, kbc, hp, expand, fold)


def row_tables(scene, live):
    total = scene.shape[0]
    far = jnp.full((TAPS - 1,), -1, scene.dtype)
    before = jnp.concatenate([far, scene])
    after = jnp.concatenate([scene, far])
    lines = [live]
    lines += [(before[TAPS - 1 - lag : TAPS - 1 - lag + total] == scene).astype(F32) for lag in range(1, TAPS)]
    lines += [(after[lag : lag + total] == scene).astype(F32) for lag in range(1, TAPS)]
    lines.append(scene.astype(F32))
    blocks = scene.reshape(total // CHUNK, CHUNK)
    last = blocks[:, -1:]
    ahead = jnp.concatenate([jnp.full((1, 1), -1, scene.dtype), last[:-1]])
    lines.append((blocks == ahead).astype(F32).reshape(total))
    lines.append((blocks == last).astype(F32).reshape(total))
    lines.append(jnp.broadcast_to((last == ahead).astype(F32), blocks.shape).reshape(total))
    table = jnp.stack(lines + [jnp.zeros((total,), F32)] * (16 - len(lines)))
    col = jnp.pad(table.T, ((0, 0), (0, LANES - 16)))
    row = jnp.broadcast_to(scene.astype(F32)[None, :], (8, total))
    return col, row


def head_tables(width):
    heads = lax.broadcasted_iota(jnp.int32, (LANES, width), 0)
    owner = lax.broadcasted_iota(jnp.int32, (LANES, width), 1) // HEAD
    expand = (heads == owner).astype(BF16)
    return expand, expand.T


def lane_row(vector):
    return jnp.pad(vector, (0, LANES - vector.shape[0]))


def swap(value, axis, size, bit):
    return lax.ppermute(value, axis, [(place, place ^ bit) for place in range(size)])


def bits(size):
    return [1 << power for power in range(size.bit_length() - 1)]


def sum_small(value, axes):
    for axis in axes:
        size = lax.axis_size(axis)
        for bit in bits(size):
            value = value + swap(value, axis, size, bit)
    return value


def sum_large(values, axis, middle):
    size = lax.axis_size(axis)
    place = lax.axis_index(axis)
    kinds = (BF16, F32)
    for bit in bits(size):
        upper = (place & bit) > 0
        halves = []
        for value, kind in zip(values, kinds):
            half = value.shape[0] // 2
            low, high = value[:half], value[half:]
            other = swap(jnp.where(upper, low, high).astype(kind), axis, size, bit)
            halves.append(jnp.where(upper, high, low) + other.astype(F32))
        values = halves
    values = [value.astype(BF16) for value in middle(values)]
    for bit in reversed(bits(size)):
        upper = (place & bit) > 0
        others = [swap(value, axis, size, bit) for value in values]
        values = [
            jnp.concatenate([jnp.where(upper, other, value), jnp.where(upper, value, other)])
            for value, other in zip(values, others)
        ]
    return [value.astype(F32) for value in values]


def shards(
    tokens, scene_ids, valid, norm_gain, w_z, w_x, w_b, w_c, w_dt, conv_x, conv_x_bias, conv_bc, conv_bc_bias,
    dt_bias, a_log, d_skip, gate_gain, w_out, cotangent,
):
    size = lax.axis_size("tensor")
    index = lax.axis_index("tensor")
    rows_own, model_width = tokens.shape
    width = w_z.shape[1]
    heads = w_dt.shape[1]
    double = 2 * w_b.shape[1]
    inner_width = width * size
    scene = scene_ids[0]
    live = valid[0].astype(F32)

    def reorder(value):
        blocks = [
            lax.dynamic_slice_in_dim(value, lax.rem(index + size - block, size) * rows_own, rows_own)
            for block in range(size)
        ]
        return jnp.concatenate(blocks)

    def rotate(value):
        return [
            lax.ppermute(value, "tensor", [(source, (source + shift) % size) for source in range(size)])
            for shift in range(1, size)
        ]

    def scatter(value):
        total = value[:rows_own].astype(F32)
        for shift in range(1, size):
            part = value[(size - shift) * rows_own : (size - shift + 1) * rows_own].astype(BF16)
            pairs = [(source, (source + shift) % size) for source in range(size)]
            total = total + lax.ppermute(part, "tensor", pairs).astype(F32)
        return total

    others = rotate(tokens)

    live_first = reorder(live)[:, None]
    live_own = live_first[:rows_own]
    col, row = row_tables(scene, live)
    expand, fold = head_tables(width)
    gain_in = norm_gain.astype(F32)[None, :]
    at = jnp.reshape(index, (1,)).astype(jnp.int32)

    def normalize(value):
        value = value.astype(F32)
        inverse = lax.rsqrt(jnp.mean(value * value, axis=1, keepdims=True) + EPSILON)
        return (value * inverse * gain_in).astype(BF16)

    w_cat = jnp.concatenate([w_x, w_b, w_c, jnp.pad(w_dt, ((0, 0), (0, LANES - heads)))], axis=1)
    normed_own = normalize(tokens)
    mine = nn(normed_own, w_cat)
    zmine = nn(normed_own, w_z)
    cot_own = cotangent * live_own.astype(BF16)
    back_own = nt(cot_own, w_out)
    mine, zmine, back_own, others, held = lax.optimization_barrier((mine, zmine, back_own, others, cotangent))
    cot_others = rotate(held)
    normed_other = normalize(jnp.concatenate(others))
    other = nn(normed_other, w_cat)
    zother = nn(normed_other, w_z)

    skip = jnp.repeat(d_skip.astype(F32), HEAD)
    gain_gate = gate_gain.astype(F32)[None, :]
    kx = jnp.concatenate(
        [conv_x.astype(F32), conv_x_bias.astype(F32)[None], skip[None], gain_gate, jnp.zeros((1, width), F32)]
    )
    kbc = jnp.concatenate([conv_bc.astype(F32), conv_bc_bias.astype(F32)[None], jnp.zeros((3, double), F32)])
    rate = -jnp.exp(a_log.astype(F32))
    hp = jnp.concatenate([lane_row(dt_bias.astype(F32))[None], lane_row(rate)[None], jnp.zeros((6, LANES), F32)])

    gated, silu, slope, xc, sp, raw, bc, spbc, step, cum, dsig, squares, states = call_forward(
        at, size, mine, other, zmine, zother, col, row, kx, kbc, hp, expand
    )
    cot_rest = jnp.concatenate(cot_others) * live_first[rows_own:].astype(BF16)
    cot_all = jnp.concatenate([cot_own, cot_rest])
    normed_grad = jnp.concatenate([back_own, nt(cot_rest, w_out)])
    gated32 = gated.astype(F32)
    dots = jnp.sum(normed_grad * gated32, axis=1)
    stats = sum_small(jnp.stack([squares[0], reorder(dots)]), ["tensor"])
    branch = nn(gated, w_out)
    inverse = reorder(lax.rsqrt(stats[0] / inner_width + EPSILON))[:, None]
    lean = inverse**3 * (reorder(stats[1]) / inner_width)[:, None]

    block_out = (tokens.astype(F32) + live_own * inverse[:rows_own] * scatter(branch)).astype(BF16)
    grad_w_out = tn(gated, (cot_all.astype(F32) * inverse).astype(BF16))

    grad_gate_gain = jnp.sum(normed_grad * gated32 * inverse, axis=0) / gain_gate[0]
    gated_grad = normed_grad * gain_gate * inverse - gated32 * lean / gain_gate
    dy = gated_grad * silu.astype(F32)
    gate_grad = (gated_grad * slope.astype(F32)).astype(BF16)
    normed = jnp.concatenate([normed_own, normed_other])
    grad_w_z = tn(normed, gate_grad)
    early = (grad_w_out.astype(BF16), grad_w_z.astype(BF16))
    early, dy = lax.optimization_barrier((early, dy))
    early = lax.psum(early, "dp")

    cat_grad, gk, gkbc, gh = call_backward(
        at, size, dy, xc, sp, raw, bc, spbc, step, cum, dsig, col, row, states, kx, kbc, hp, expand, fold
    )
    grad_cat = lax.optimization_barrier(tn(normed, cat_grad))

    def shared_columns(values):
        part = values[1][:, :double]
        for bit in bits(size):
            part = part + swap(part, "tensor", size, bit)
        return [values[0], jnp.concatenate([part, values[1][:, double:]], axis=1)]

    late, rest = sum_large([grad_cat[:, :width], grad_cat[:, width:]], "dp", shared_columns)
    back = nt(gate_grad, w_z) + nt(cat_grad, w_cat)
    normed_in_grad = scatter(back)

    weighted = grad_cat * w_cat.astype(F32)
    norm_part = jnp.sum(weighted, axis=1) + jnp.sum(grad_w_z * w_z.astype(F32), axis=1)
    gk = gk.reshape(TAPS + 2, 8, width).sum(1)
    gkbc = gkbc.reshape(TAPS + 1, 8, double).sum(1)
    gh = gh.reshape(2, 8, LANES).sum(1)
    g_skip = gk[TAPS + 1].reshape(heads, HEAD).sum(1)
    local = jnp.concatenate([gk[: TAPS + 1].reshape(-1), grad_gate_gain, gh.reshape(-1), lane_row(g_skip)])
    shared = jnp.concatenate([norm_part / norm_gain.astype(F32), gkbc.reshape(-1)])
    cut = local.shape[0]
    small = jnp.concatenate([local, shared])
    small = jnp.pad(small, (0, -small.shape[0] % 1024)).reshape(-1, LANES)
    small = sum_small(small, ["dp"]).reshape(-1)
    local = small[:cut]
    shared = sum_small(small[cut:].reshape(-1, LANES), ["tensor"]).reshape(-1)
    taps = local[: (TAPS + 1) * width].reshape(TAPS + 1, width)
    local = local[(TAPS + 1) * width :]
    taps_bc = shared[model_width : model_width + (TAPS + 1) * double].reshape(TAPS + 1, double)

    resid = tokens.astype(F32)
    inverse_in = lax.rsqrt(jnp.mean(resid * resid, axis=1, keepdims=True) + EPSILON)
    inner = jnp.sum(gain_in * normed_in_grad * resid, axis=1, keepdims=True)
    grad_tokens = (
        cotangent.astype(F32)
        + inverse_in * gain_in * normed_in_grad
        - resid * inverse_in**3 * (inner / model_width)
    ).astype(BF16)
    return (
        block_out,
        grad_tokens,
        shared[:model_width],
        early[1].astype(F32),
        late,
        rest[:, : double // 2],
        rest[:, double // 2 : double],
        rest[:, double : double + heads],
        taps[:TAPS],
        taps[TAPS],
        taps_bc[:TAPS],
        taps_bc[TAPS],
        local[width : width + heads],
        local[width + LANES : width + LANES + heads],
        local[width + 2 * LANES : width + 2 * LANES + heads],
        local[:width],
        early[0].astype(F32),
    )


def solution(mesh):
    own = P(("dp", "tensor"), None)
    packs, both = P("dp", None), P()
    cols, vector = P(None, "tensor"), P("tensor")
    in_specs = (
        own, packs, packs, both, cols, cols, both, both, cols, cols, vector, both, both,
        vector, vector, vector, vector, P("tensor", None), own,
    )
    out_specs = (
        own, own, both, cols, cols, both, both, cols, cols, vector, both, both,
        vector, vector, vector, vector, P("tensor", None),
    )
    return jax.shard_map(shards, mesh=mesh, in_specs=in_specs, out_specs=out_specs, check_vma=False)
```

```python
import functools

import jax
import jax.numpy as jnp
from jax import lax
from jax.experimental import pallas as pl
from jax.experimental.pallas import tpu as pltpu
from jax.sharding import PartitionSpec as P

EPSILON = 1e-05
HEAD = 64
LANES = 128
CHUNK = 128
TAPS = 4
FAR = -1e30
F32 = jnp.float32
BF16 = jnp.bfloat16
HIGHEST = lax.Precision.HIGHEST

LIVE, PREV, NEXT, SCENE, CARRIED, TAIL, KEEP = 0, 1, 4, 7, 8, 9, 10


def nn(left, right):
    return jnp.dot(left, right, preferred_element_type=F32)


def nt(left, right):
    return lax.dot_general(left, right, (((1,), (1,)), ((), ())), preferred_element_type=F32)


def split(value):
    high = value.astype(BF16)
    return high, (value - high.astype(F32)).astype(BF16)


def fine(product, left, right):
    left_high, left_low = split(left)
    right_high, right_low = split(right)
    return product(left_high, right_high) + (product(left_high, right_low) + product(left_low, right_high))


def tn(left, right):
    return lax.dot_general(left, right, (((0,), (0,)), ((), ())), preferred_element_type=F32)


def sigmoid(value):
    return 1.0 / (1.0 + jnp.exp(-value))


def softplus(value):
    small = jnp.exp(-jnp.abs(value))
    shifted = 1.0 + small
    tiny = shifted == 1.0
    ratio = jnp.log(shifted) * small / jnp.where(tiny, 1.0, shifted - 1.0)
    return jnp.maximum(value, 0.0) + jnp.where(tiny, small, ratio)


def spread(rows, table):
    high, low = split(rows)
    return nn(high, table) + nn(low, table)


def fold8(value):
    return jnp.sum(value.reshape(value.shape[0] // 8, 8, value.shape[1]), axis=0)


def head_pair(value):
    lane = lax.broadcasted_iota(jnp.int32, value.shape, 1)
    zero = jnp.zeros_like(value)
    return jnp.concatenate(
        [jnp.where(lane < HEAD, value, zero), jnp.where(lane < HEAD, zero, value)], axis=0
    )


def forward_kernel(
    per_block, at_ref, mine_ref, other_ref, zmine_ref, zother_ref, col_ref, row_ref, kx_ref, kbc_ref, hp_ref, ex_ref,
    gated_ref, silu_ref, slope_ref, xc_ref, sp_ref, raw_ref, bc_ref, spbc_ref, dt_ref, cum_ref, ds_ref, sq_ref, st_ref,
    xs, gs, state,
):
    rows, width = xc_ref.shape
    double = bc_ref.shape[1]
    count = double // 2
    own = pl.program_id(0) // per_block == at_ref[0]

    @pl.when(pl.program_id(0) == 0)
    def _():
        xs[0:8, :] = jnp.zeros((8, xs.shape[1]), F32)
        state[...] = jnp.zeros_like(state)

    @pl.when(own)
    def _():
        xs[8:, :] = mine_ref[...]
        gs[...] = zmine_ref[...]

    @pl.when(jnp.logical_not(own))
    def _():
        xs[8:, :] = other_ref[...]
        gs[...] = zother_ref[...]

    raw_ref[...] = xs[8:, : width + double].astype(BF16)
    live = col_ref[:, LIVE : LIVE + 1]
    same = [col_ref[:, PREV + lag : PREV + lag + 1] for lag in range(TAPS - 1)]

    side = slice(width, width + double)
    raw = xs[8:, side]
    pre = kbc_ref[TAPS : TAPS + 1, :] + kbc_ref[TAPS - 1 : TAPS, :] * raw
    for lag in range(1, TAPS):
        tap = kbc_ref[TAPS - 1 - lag : TAPS - lag, :]
        pre = pre + tap * (xs[8 - lag : 8 - lag + rows, side] * same[lag - 1])
    sig = sigmoid(pre)
    act = pre * sig
    spbc_ref[...] = (sig * (1.0 + pre * (1.0 - sig))).astype(spbc_ref.dtype)
    bc_ref[...] = act
    act16 = act.astype(BF16)
    b16 = act16[:, :count]
    c16 = act16[:, count:]

    biased = xs[8:, width + double :] + hp_ref[0:1, :]
    ds_ref[...] = sigmoid(biased) * live
    step = softplus(biased) * live
    dt_ref[...] = step
    decay = step * hp_ref[1:2, :]
    above = lax.broadcasted_iota(jnp.int32, (rows, rows), 0)
    along = lax.broadcasted_iota(jnp.int32, (rows, rows), 1)
    lower = above >= along
    cum = jnp.dot(lower.astype(F32), decay, precision=HIGHEST, preferred_element_type=F32)
    cum_ref[...] = cum
    cum_t = cum.T
    last = cum[rows - 1 : rows, :]
    from_start = jnp.exp(cum) * col_ref[:, CARRIED : CARRIED + 1]
    to_end = jnp.exp(last - cum) * col_ref[:, TAIL : TAIL + 1]
    keep = jnp.exp(last) * col_ref[0:1, KEEP : KEEP + 1]
    table = ex_ref[...]
    wide = spread(jnp.concatenate([step, from_start, to_end, jnp.broadcast_to(keep, (8, LANES))], axis=0), table)

    mask = lower & (col_ref[:, SCENE : SCENE + 1] == row_ref[0:1, :])
    scores = nt(c16, b16)
    b_t = act[:, :count].T
    squares = jnp.zeros((rows, LANES), F32)
    for group in range(width // LANES):
        part = slice(group * LANES, (group + 1) * LANES)
        pre = kx_ref[TAPS : TAPS + 1, part] + kx_ref[TAPS - 1 : TAPS, part] * xs[8:, part]
        for lag in range(1, TAPS):
            tap = kx_ref[TAPS - 1 - lag : TAPS - lag, part]
            pre = pre + tap * (xs[8 - lag : 8 - lag + rows, part] * same[lag - 1])
        sig = sigmoid(pre)
        xc = pre * sig * live
        xc_ref[:, part] = xc
        sp_ref[:, part] = (sig * (1.0 + pre * (1.0 - sig)) * live).astype(BF16)
        both = []
        for head in (2 * group, 2 * group + 1):
            gap = cum[:, head : head + 1] - cum_t[head : head + 1, :]
            weight = jnp.exp(jnp.where(mask, gap, FAR))
            both.append((weight * scores).astype(BF16))
        stepped = xc * wide[:rows, part]
        inner = nn(jnp.concatenate(both, axis=1), head_pair(stepped.astype(BF16)))
        old = state[:, part]
        old16 = old.astype(BF16)
        st_ref[0, :, part] = old
        mixed = inner + nn(c16, old16) * wide[rows : 2 * rows, part] + kx_ref[TAPS + 1 : TAPS + 2, part] * xc
        fed = stepped * wide[2 * rows : 3 * rows, part]
        state[:, part] = old * wide[3 * rows : 3 * rows + 1, part] + fine(nn, b_t, fed)
        gate = gs[:, part]
        sig = sigmoid(gate)
        silu = gate * sig
        gated = mixed * silu
        gated_ref[:, part] = (gated * kx_ref[TAPS + 2 : TAPS + 3, part]).astype(BF16)
        silu_ref[:, part] = silu.astype(BF16)
        slope_ref[:, part] = (mixed * sig * (1.0 + gate * (1.0 - sig))).astype(BF16)
        squares = squares + gated * gated
    sq_ref[...] = nt(jnp.ones((8, LANES), BF16), squares.astype(BF16))
    xs[0:8, :] = xs[rows : rows + 8, :]


def backward_kernel(
    at_ref, dy_ref, xc_ref, sp_ref, x_ref, bc_ref, spbc_ref, dt_ref, cum_ref, ds_ref, col_ref, row_ref,
    st_ref, kx_ref, kbc_ref, hp_ref, ex_ref, fo_ref,
    out_ref, gk_ref, gkbc_ref, gh_ref,
    dvs, dbs, grad, rowsum,
):
    rows, width = xc_ref.shape
    double = bc_ref.shape[1]
    count = double // 2

    @pl.when(pl.program_id(0) == 0)
    def _():
        dvs[rows:, :] = jnp.zeros((8, width), F32)
        dbs[rows:, :] = jnp.zeros((8, double), F32)
        grad[...] = jnp.zeros_like(grad)
        rowsum[...] = jnp.zeros_like(rowsum)
        gk_ref[...] = jnp.zeros_like(gk_ref)
        gkbc_ref[...] = jnp.zeros_like(gkbc_ref)
        gh_ref[...] = jnp.zeros_like(gh_ref)

    @pl.when(pl.program_id(0) > 0)
    def _():
        dvs[rows:, :] = dvs[0:8, :]
        dbs[rows:, :] = dbs[0:8, :]

    same = [col_ref[:, NEXT + lag : NEXT + lag + 1] for lag in range(TAPS - 1)]
    b = bc_ref[:, :count]
    c = bc_ref[:, count:]
    step = dt_ref[...]
    cum = cum_ref[...]
    cum_t = cum.T
    last = cum[rows - 1 : rows, :]
    from_start = jnp.exp(cum) * col_ref[:, CARRIED : CARRIED + 1]
    to_end = jnp.exp(last - cum) * col_ref[:, TAIL : TAIL + 1]
    keep = jnp.exp(last) * col_ref[0:1, KEEP : KEEP + 1]
    table = ex_ref[...]
    wide = spread(jnp.concatenate([step, from_start, to_end, jnp.broadcast_to(keep, (8, LANES))], axis=0), table)

    above = lax.broadcasted_iota(jnp.int32, (rows, rows), 0)
    along = lax.broadcasted_iota(jnp.int32, (rows, rows), 1)
    upper = above <= along
    mask = upper & (col_ref[:, SCENE : SCENE + 1] == row_ref[0:1, :])
    scores = fine(nt, b, c)
    c_t = c.T
    lane = lax.broadcasted_iota(jnp.int32, (rows, LANES), 1)

    d_scores = jnp.zeros((rows, rows), F32)
    d_b = jnp.zeros((rows, count), F32)
    d_c = jnp.zeros((rows, count), F32)
    d_cum = jnp.zeros((rows, LANES), F32)
    d_step = jnp.zeros((rows, LANES), F32)
    d_last = jnp.zeros((8, LANES), F32)
    for group in range(width // LANES):
        part = slice(group * LANES, (group + 1) * LANES)
        dy = dy_ref[:, part]
        xc = xc_ref[:, part]
        wide_step = wide[:rows, part]
        wide_end = wide[2 * rows : 3 * rows, part]
        fold = fo_ref[part, :]
        pair = head_pair(dy)
        stepped = xc * wide_step
        back = fine(nt, stepped, pair)
        both = []
        for which, head in enumerate((2 * group, 2 * group + 1)):
            gap = cum_t[head : head + 1, :] - cum[:, head : head + 1]
            weight = jnp.exp(jnp.where(mask, gap, FAR))
            both.append(weight * scores)
            weighted = back[:, which * rows : (which + 1) * rows] * weight
            d_scores = d_scores + weighted
            inner = weighted * scores
            rowsum[head : head + 1, :] = jnp.sum(inner, axis=0, keepdims=True)
            d_cum = d_cum - jnp.where(lane == head, jnp.sum(inner, axis=1, keepdims=True), 0.0)
        d_stepped = fine(nn, jnp.concatenate(both, axis=1), pair)
        old = st_ref[0, :, part]
        after = grad[:, part]
        carried = dy * wide[rows : 2 * rows, part]
        fed = stepped * wide_end
        from_after = fine(nn, b, after)
        to_last = fed * from_after
        d_b = d_b + fine(nt, fed, after)
        d_c = d_c + fine(nt, carried, old)
        d_cum = d_cum + spread(carried * fine(nn, c, old) - to_last, fold)
        kept = wide[3 * rows : 3 * rows + 1, part]
        total = fold8(to_last) + fold8(after * old) * kept
        d_last = d_last + spread(total, fold)
        grad[:, part] = after * kept + fine(nn, c_t, carried)
        d_stepped = d_stepped + from_after * wide_end
        d_xc = d_stepped * wide_step + kx_ref[TAPS + 1 : TAPS + 2, part] * dy
        d_step = d_step + spread(d_stepped * xc, fold)
        dv = d_xc * sp_ref[:, part].astype(F32)
        dvs[0:rows, part] = dv
        x = x_ref[:, part].astype(F32)
        xg = kx_ref[TAPS - 1 : TAPS, part] * dv
        gk_ref[8 * (TAPS - 1) : 8 * TAPS, part] += fold8(x * dv)
        gk_ref[8 * TAPS : 8 * TAPS + 8, part] += fold8(dv)
        gk_ref[8 * TAPS + 8 : 8 * TAPS + 16, part] += fold8(dy * xc)
        for lag in range(1, TAPS):
            moved = dvs[lag : lag + rows, part] * same[lag - 1]
            xg = xg + kx_ref[TAPS - 1 - lag : TAPS - lag, part] * moved
            gk_ref[8 * (TAPS - 1 - lag) : 8 * (TAPS - lag), part] += fold8(x * moved)
        out_ref[:, part] = xg.astype(BF16)

    d_b = d_b + fine(nn, d_scores, c)
    d_c = d_c + fine(nn, d_scores.T, b)
    for side, value in ((0, d_b), (1, d_c)):
        part = slice(side * count, (side + 1) * count)
        dv = value * spbc_ref[:, part].astype(F32)
        dbs[0:rows, part] = dv
        raw = x_ref[:, width + side * count : width + (side + 1) * count].astype(F32)
        out = kbc_ref[TAPS - 1 : TAPS, part] * dv
        gkbc_ref[8 * (TAPS - 1) : 8 * TAPS, part] += fold8(raw * dv)
        gkbc_ref[8 * TAPS : 8 * TAPS + 8, part] += fold8(dv)
        for lag in range(1, TAPS):
            moved = dbs[lag : lag + rows, part] * same[lag - 1]
            out = out + kbc_ref[TAPS - 1 - lag : TAPS - lag, part] * moved
            gkbc_ref[8 * (TAPS - 1 - lag) : 8 * (TAPS - lag), part] += fold8(raw * moved)
        out_ref[:, width + side * count : width + (side + 1) * count] = out.astype(BF16)

    d_cum = d_cum + rowsum[...].T
    d_decay = jnp.dot(upper.astype(F32), d_cum, precision=HIGHEST, preferred_element_type=F32)
    d_decay = d_decay + jnp.sum(d_last, axis=0, keepdims=True)
    d_step = d_step + d_decay * hp_ref[1:2, :]
    d_raw = d_step * ds_ref[...]
    gh_ref[0:8, :] += fold8(d_raw)
    gh_ref[8:16, :] += fold8(d_decay * step * hp_ref[1:2, :])
    out_ref[:, width + double :] = d_raw.astype(BF16)


def physical(step, at, size, per_block):
    return lax.rem(at - step // per_block + size, size) * per_block + lax.rem(step, per_block)


def call_forward(at, size, mine, other, zmine, zother, col, row, kx, kbc, hp, expand):
    cat = mine.shape[1]
    width = zmine.shape[1]
    double = cat - width - LANES
    total = mine.shape[0] * size
    steps = total // CHUNK
    per_block = mine.shape[0] // CHUNK

    def own_place(i, at_ref):
        return jnp.clip(i - at_ref[0] * per_block, 0, per_block - 1), 0

    def other_place(i, at_ref):
        place = physical(i, at_ref[0], size, per_block) - per_block
        resting = jnp.where(at_ref[0] == 0, (size - 2) * per_block, per_block - 1)
        return jnp.where(place < 0, resting, place), 0

    def rows(cols):
        return pl.BlockSpec((CHUNK, cols), lambda i, at_ref: (i, 0))

    def moved(cols):
        return pl.BlockSpec((CHUNK, cols), lambda i, at_ref: (physical(i, at_ref[0], size, per_block), 0))

    def whole(array):
        return pl.BlockSpec(array.shape, lambda i, at_ref: (0, 0))

    lanes8 = pl.BlockSpec((8, CHUNK), lambda i, at_ref: (0, i))
    shape = jax.ShapeDtypeStruct
    return pl.pallas_call(
        functools.partial(forward_kernel, per_block),
        grid_spec=pltpu.PrefetchScalarGridSpec(
            num_scalar_prefetch=1,
            grid=(steps,),
            in_specs=[
                pl.BlockSpec((CHUNK, cat), own_place), pl.BlockSpec((CHUNK, cat), other_place),
                pl.BlockSpec((CHUNK, width), own_place), pl.BlockSpec((CHUNK, width), other_place),
                rows(LANES), lanes8, whole(kx), whole(kbc), whole(hp), whole(expand),
            ],
            out_specs=[
                moved(width), moved(width), moved(width), rows(width), rows(width), rows(width + double),
                rows(double), rows(double), rows(LANES), rows(LANES), rows(LANES), lanes8,
                pl.BlockSpec((1, double // 2, width), lambda i, at_ref: (i, 0, 0)),
            ],
            scratch_shapes=[
                pltpu.VMEM((CHUNK + 8, cat), F32),
                pltpu.VMEM((CHUNK, width), F32),
                pltpu.VMEM((double // 2, width), F32),
            ],
        ),
        out_shape=[
            shape((total, width), BF16), shape((total, width), BF16), shape((total, width), BF16),
            shape((total, width), F32), shape((total, width), BF16), shape((total, width + double), BF16),
            shape((total, double), F32), shape((total, double), BF16),
            shape((total, LANES), F32), shape((total, LANES), F32), shape((total, LANES), F32), shape((8, total), F32),
            shape((steps, double // 2, width), F32),
        ],
        name="scan_forward",
    )(at, mine, other, zmine, zother, col, row, kx, kbc, hp, expand)


def call_backward(at, size, dy, xc, sp, raw, bc, spbc, step, cum, dsig, col, row, states, kx, kbc, hp, expand, fold):
    total, width = xc.shape
    double = bc.shape[1]
    cat = width + double + LANES
    steps = total // CHUNK
    per_block = steps // size

    def rows(cols):
        return pl.BlockSpec((CHUNK, cols), lambda i, at_ref: (steps - 1 - i, 0))

    def moved(cols):
        return pl.BlockSpec((CHUNK, cols), lambda i, at_ref: (physical(steps - 1 - i, at_ref[0], size, per_block), 0))

    def whole(array):
        return pl.BlockSpec(array.shape, lambda i, at_ref: (0, 0))

    lanes8 = pl.BlockSpec((8, CHUNK), lambda i, at_ref: (0, steps - 1 - i))
    shape = jax.ShapeDtypeStruct
    sums = [shape((8 * (TAPS + 2), width), F32), shape((8 * (TAPS + 1), double), F32), shape((16, LANES), F32)]
    return pl.pallas_call(
        backward_kernel,
        grid_spec=pltpu.PrefetchScalarGridSpec(
            num_scalar_prefetch=1,
            grid=(steps,),
            in_specs=[
                moved(width), rows(width), rows(width), rows(width + double),
                rows(double), rows(double), rows(LANES), rows(LANES), rows(LANES), rows(LANES), lanes8,
                pl.BlockSpec((1, double // 2, width), lambda i, at_ref: (steps - 1 - i, 0, 0)),
                whole(kx), whole(kbc), whole(hp), whole(expand), whole(fold),
            ],
            out_specs=[moved(cat)] + [whole(member) for member in sums],
            scratch_shapes=[
                pltpu.VMEM((CHUNK + 8, width), F32),
                pltpu.VMEM((CHUNK + 8, double), F32),
                pltpu.VMEM((double // 2, width), F32),
                pltpu.VMEM((LANES, CHUNK), F32),
            ],
        ),
        out_shape=[shape((total, cat), BF16)] + sums,
        name="scan_backward",
    )(at, dy, xc, sp, raw, bc, spbc, step, cum, dsig, col, row, states, kx, kbc, hp, expand, fold)


def row_tables(scene, live):
    total = scene.shape[0]
    far = jnp.full((TAPS - 1,), -1, scene.dtype)
    before = jnp.concatenate([far, scene])
    after = jnp.concatenate([scene, far])
    lines = [live]
    lines += [(before[TAPS - 1 - lag : TAPS - 1 - lag + total] == scene).astype(F32) for lag in range(1, TAPS)]
    lines += [(after[lag : lag + total] == scene).astype(F32) for lag in range(1, TAPS)]
    lines.append(scene.astype(F32))
    blocks = scene.reshape(total // CHUNK, CHUNK)
    last = blocks[:, -1:]
    ahead = jnp.concatenate([jnp.full((1, 1), -1, scene.dtype), last[:-1]])
    lines.append((blocks == ahead).astype(F32).reshape(total))
    lines.append((blocks == last).astype(F32).reshape(total))
    lines.append(jnp.broadcast_to((last == ahead).astype(F32), blocks.shape).reshape(total))
    table = jnp.stack(lines + [jnp.zeros((total,), F32)] * (16 - len(lines)))
    col = jnp.pad(table.T, ((0, 0), (0, LANES - 16)))
    row = jnp.broadcast_to(scene.astype(F32)[None, :], (8, total))
    return col, row


def head_tables(width):
    heads = lax.broadcasted_iota(jnp.int32, (LANES, width), 0)
    owner = lax.broadcasted_iota(jnp.int32, (LANES, width), 1) // HEAD
    expand = (heads == owner).astype(BF16)
    return expand, expand.T


def lane_row(vector):
    return jnp.pad(vector, (0, LANES - vector.shape[0]))


def swap(value, axis, size, bit):
    return lax.ppermute(value, axis, [(place, place ^ bit) for place in range(size)])


def bits(size):
    return [1 << power for power in range(size.bit_length() - 1)]


def sum_small(value, axes):
    for axis in axes:
        size = lax.axis_size(axis)
        for bit in bits(size):
            value = value + swap(value, axis, size, bit)
    return value


def halves(low, high, axis, bit):
    upper = (lax.axis_index(axis) & bit) > 0
    other = swap(jnp.where(upper, low, high).astype(BF16), axis, lax.axis_size(axis), bit)
    return jnp.where(upper, high, low) + other.astype(F32)


def join(value, axis, bit):
    upper = (lax.axis_index(axis) & bit) > 0
    other = swap(value, axis, lax.axis_size(axis), bit)
    return jnp.where(upper, other, value), jnp.where(upper, value, other)


def sum_rest(value, axis, held):
    size = lax.axis_size(axis)
    groups = size // 4
    place = lax.axis_index(axis) // 4
    half = value.shape[0] // 2
    value = halves(value[:half], value[half:], axis, 2)
    rows = half // groups

    def piece(owner):
        return lax.dynamic_slice_in_dim(value, owner * rows, rows)

    sent = [piece(place ^ offset).astype(BF16) for offset in range(1, groups)]
    total = piece(place)
    for offset, member in zip(range(1, groups), sent):
        total = total + swap(member, axis, size, 4 * offset).astype(F32)
    total, held = lax.optimization_barrier((total.astype(BF16), held))
    pieces = [total] + [swap(total, axis, size, 4 * offset) for offset in range(1, groups)]
    for bit in bits(groups):
        moved = (place & bit) > 0
        pieces = [jnp.where(moved, pieces[at ^ bit], pieces[at]) for at in range(groups)]
    return jnp.concatenate(join(jnp.concatenate(pieces), axis, 2)), held


def shards(
    tokens, scene_ids, valid, norm_gain, w_z, w_x, w_b, w_c, w_dt, conv_x, conv_x_bias, conv_bc, conv_bc_bias,
    dt_bias, a_log, d_skip, gate_gain, w_out, cotangent,
):
    size = lax.axis_size("tensor")
    index = lax.axis_index("tensor")
    rows_own, model_width = tokens.shape
    width = w_z.shape[1]
    heads = w_dt.shape[1]
    double = 2 * w_b.shape[1]
    inner_width = width * size
    scene = scene_ids[0]
    live = valid[0].astype(F32)

    def reorder(value):
        blocks = [
            lax.dynamic_slice_in_dim(value, lax.rem(index + size - block, size) * rows_own, rows_own)
            for block in range(size)
        ]
        return jnp.concatenate(blocks)

    def rotate(value):
        return [
            lax.ppermute(value, "tensor", [(source, (source + shift) % size) for source in range(size)])
            for shift in range(1, size)
        ]

    def scatter(value):
        total = value[:rows_own].astype(F32)
        for shift in range(1, size):
            part = value[(size - shift) * rows_own : (size - shift + 1) * rows_own].astype(BF16)
            pairs = [(source, (source + shift) % size) for source in range(size)]
            total = total + lax.ppermute(part, "tensor", pairs).astype(F32)
        return total

    others = rotate(tokens)

    live_first = reorder(live)[:, None]
    live_own = live_first[:rows_own]
    col, row = row_tables(scene, live)
    expand, fold = head_tables(width)
    gain_in = norm_gain.astype(F32)[None, :]
    at = jnp.reshape(index, (1,)).astype(jnp.int32)

    def normalize(value):
        value = value.astype(F32)
        inverse = lax.rsqrt(jnp.mean(value * value, axis=1, keepdims=True) + EPSILON)
        return (value * inverse * gain_in).astype(BF16)

    w_cat = jnp.concatenate([w_x, w_b, w_c, jnp.pad(w_dt, ((0, 0), (0, LANES - heads)))], axis=1)
    normed_own = normalize(tokens)
    mine = nn(normed_own, w_cat)
    zmine = nn(normed_own, w_z)
    cot_own = cotangent * live_own.astype(BF16)
    back_own = nt(cot_own, w_out)
    mine, zmine, back_own, others, held = lax.optimization_barrier((mine, zmine, back_own, others, cotangent))
    cot_others = rotate(held)
    normed_other = normalize(jnp.concatenate(others))
    other = nn(normed_other, w_cat)
    zother = nn(normed_other, w_z)

    skip = jnp.repeat(d_skip.astype(F32), HEAD)
    gain_gate = gate_gain.astype(F32)[None, :]
    kx = jnp.concatenate(
        [conv_x.astype(F32), conv_x_bias.astype(F32)[None], skip[None], gain_gate, jnp.zeros((1, width), F32)]
    )
    kbc = jnp.concatenate([conv_bc.astype(F32), conv_bc_bias.astype(F32)[None], jnp.zeros((3, double), F32)])
    rate = -jnp.exp(a_log.astype(F32))
    hp = jnp.concatenate([lane_row(dt_bias.astype(F32))[None], lane_row(rate)[None], jnp.zeros((6, LANES), F32)])

    gated, silu, slope, xc, sp, raw, bc, spbc, step, cum, dsig, squares, states = call_forward(
        at, size, mine, other, zmine, zother, col, row, kx, kbc, hp, expand
    )
    cot_rest = jnp.concatenate(cot_others) * live_first[rows_own:].astype(BF16)
    cot_all = jnp.concatenate([cot_own, cot_rest])
    back_rest = nt(cot_rest, w_out)
    normed_grad = jnp.concatenate([back_own, back_rest])
    gated32 = gated.astype(F32)
    dots = jnp.sum(normed_grad * gated32, axis=1)
    stats = sum_small(jnp.stack([squares[0], reorder(dots)]), ["tensor"])
    branch = nn(gated, w_out)
    inverse = reorder(lax.rsqrt(stats[0] / inner_width + EPSILON))[:, None]
    lean = inverse**3 * (reorder(stats[1]) / inner_width)[:, None]

    branch = scatter(branch)
    grad_w_out = tn(gated, (cot_all.astype(F32) * inverse).astype(BF16))

    gated_grad = normed_grad * gain_gate * inverse - gated32 * lean / gain_gate
    dy = gated_grad * silu.astype(F32)
    gate_grad = (gated_grad * slope.astype(F32)).astype(BF16)
    normed = jnp.concatenate([normed_own, normed_other])
    grad_w_z = tn(normed, gate_grad)
    early = (grad_w_out.astype(BF16), grad_w_z.astype(BF16))
    early, dy, gate_grad, back_own, back_rest, gated, inverse = lax.optimization_barrier(
        (early, dy, gate_grad, back_own, back_rest, gated, inverse)
    )
    back = nt(gate_grad, w_z)
    normed_grad = jnp.concatenate([back_own, back_rest])
    grad_gate_gain = jnp.sum(normed_grad * gated.astype(F32) * inverse, axis=0) / gain_gate[0]
    norm_part = jnp.sum(early[1].astype(F32) * w_z.astype(F32), axis=1)
    dy, back, grad_gate_gain, norm_part = lax.optimization_barrier((dy, back, grad_gate_gain, norm_part))
    early = lax.psum(early, "dp")

    cat_grad, gk, gkbc, gh = call_backward(
        at, size, dy, xc, sp, raw, bc, spbc, step, cum, dsig, col, row, states, kx, kbc, hp, expand, fold
    )
    early, cat_grad, back, grad_gate_gain, norm_part, branch = lax.optimization_barrier(
        (early, cat_grad, back, grad_gate_gain, norm_part, branch)
    )
    block_out = (tokens.astype(F32) + live_own * inverse[:rows_own] * branch).astype(BF16)
    grad_cat = tn(normed, cat_grad)
    half = model_width // 2
    late = halves(grad_cat[:half], grad_cat[half:], "dp", 1)
    part = late[:, width : width + double]
    for bit in bits(size):
        part = part + swap(part, "tensor", size, bit)
    late = jnp.concatenate([late[:, :width], part, late[:, width + double :]], axis=1)
    back = back + nt(cat_grad, w_cat)
    late, back, grad_cat = lax.optimization_barrier((late, back, grad_cat))
    normed_in_grad = scatter(back)
    weighted = grad_cat * w_cat.astype(F32)
    norm_part = norm_part + jnp.sum(weighted, axis=1)
    gk = gk.reshape(TAPS + 2, 8, width).sum(1)
    gkbc = gkbc.reshape(TAPS + 1, 8, double).sum(1)
    gh = gh.reshape(2, 8, LANES).sum(1)
    g_skip = gk[TAPS + 1].reshape(heads, HEAD).sum(1)
    local = jnp.concatenate([gk[: TAPS + 1].reshape(-1), grad_gate_gain, gh.reshape(-1), lane_row(g_skip)])
    shared = jnp.concatenate([norm_part / norm_gain.astype(F32), gkbc.reshape(-1)])
    cut = local.shape[0]
    small = jnp.concatenate([local, shared])
    small = jnp.pad(small, (0, -small.shape[0] % 1024)).reshape(-1, LANES)
    late, (small, normed_in_grad) = sum_rest(late, "dp", (small, normed_in_grad))
    late = join(late, "dp", 1)
    small = sum_small(small, ["dp"]).reshape(-1)
    local = small[:cut]
    shared = sum_small(small[cut:].reshape(-1, LANES), ["tensor"]).reshape(-1)
    taps = local[: (TAPS + 1) * width].reshape(TAPS + 1, width)
    local = local[(TAPS + 1) * width :]
    taps_bc = shared[model_width : model_width + (TAPS + 1) * double].reshape(TAPS + 1, double)

    resid = tokens.astype(F32)
    inverse_in = lax.rsqrt(jnp.mean(resid * resid, axis=1, keepdims=True) + EPSILON)
    inner = jnp.sum(gain_in * normed_in_grad * resid, axis=1, keepdims=True)
    grad_tokens = (
        cotangent.astype(F32)
        + inverse_in * gain_in * normed_in_grad
        - resid * inverse_in**3 * (inner / model_width)
    ).astype(BF16)
    return (
        block_out,
        grad_tokens,
        shared[:model_width],
        early[1].astype(F32),
        jnp.concatenate([member[:, :width] for member in late]).astype(F32),
        jnp.concatenate([member[:, width : width + double // 2] for member in late]).astype(F32),
        jnp.concatenate([member[:, width + double // 2 : width + double] for member in late]).astype(F32),
        jnp.concatenate([member[:, width + double : width + double + heads] for member in late]).astype(F32),
        taps[:TAPS],
        taps[TAPS],
        taps_bc[:TAPS],
        taps_bc[TAPS],
        local[width : width + heads],
        local[width + LANES : width + LANES + heads],
        local[width + 2 * LANES : width + 2 * LANES + heads],
        local[:width],
        early[0].astype(F32),
    )


def solution(mesh):
    own = P(("dp", "tensor"), None)
    packs, both = P("dp", None), P()
    cols, vector = P(None, "tensor"), P("tensor")
    in_specs = (
        own, packs, packs, both, cols, cols, both, both, cols, cols, vector, both, both,
        vector, vector, vector, vector, P("tensor", None), own,
    )
    out_specs = (
        own, own, both, cols, cols, both, both, cols, cols, vector, both, both,
        vector, vector, vector, vector, P("tensor", None),
    )
    return jax.shard_map(shards, mesh=mesh, in_specs=in_specs, out_specs=out_specs, check_vma=False)
```
